32 devices in a mesh: group: 2 (over x), dev: 16 (over z, y, core).
Axes of the slice: x: 2, y: 2, z: 4, core: 2. Of those that a mesh axis runs over, the one named last changes fastest.
Arguments:
- positions: float32 [256, 3, 544], P(('group', 'dev')), may hold values from -6 to 6
- analysis: float32 [289, 544], replicated, may hold values from -0.25 to 0.25
- synthesis: float32 [544, 289], replicated, may hold values from -0.375 to 0.375
- stiffness: float32 [289], replicated, may hold values from 0.1 to 10
- owner: int32 [1088, 1], P(('group', 'dev')), may hold values from 0 to 15; in each aligned block of 34 rows (0 to 33, 34 to 67, ...) at most 4 rows name the same one
- ulist: int32 [2048, 4], P(('group', 'dev')), may hold values from 0 to 191, as said below
Outputs:
- moved: float32 [256, 3, 544], P(('group', 'dev'))
- velocity: float32 [256, 3, 544], P(('group', 'dev'))
The draws below stay inside these ranges and needn't reach their ends.
Inputs may be any that keep to these rules, and one draw needn't show every extreme that they name: On the points of one device, no owner receives more than 4 blocks, and some owner receives exactly 4. `ulist`: entry 0 of row r is 64 + r % 64, the slot itself.
All inputs are finite; a program needn't handle non-finite values.
Results may differ from the reference program's by a relative error of at most 0.00011.
Values sent between devices are 32-bit elements; how exact they have to be, the bound alone decides.
A program may use at most 64 MiB of HBM per device.

```python
import math
import jax
import jax.numpy as jnp
import numpy as np
from jax import lax

P_SIZE = 544
NCOEF = 289
LEAF = 128
KNEAR = 4
STEPS = 1
C_DEV = 8
CELLS = 256
BLK_DEV = 34
NBLK = 1088
CAP = 4
SLOTS = 64
LIST_ROWS = 2048
N_GROUP = 2
N_DEV = 16


def draw_ulist(key, part):
    row_ids = jnp.arange(LIST_ROWS, dtype=jnp.int32)
    others = jax.random.randint(jax.random.fold_in(key, 11), (LIST_ROWS, KNEAR - 1), 0, 3 * SLOTS, dtype=jnp.int32)
    own_column = (SLOTS + row_ids % SLOTS)[:, None]
    listed = jnp.concatenate([own_column, others], axis=1)
    listed = listed.at[0, 1].set(0)
    listed = listed.at[LIST_ROWS - 1, KNEAR - 1].set(3 * SLOTS - 1)
    return listed.astype(jnp.int32)


def block_scale(key, shape, pieces, low, largest):
    gain, own = 1.0, jax.random.fold_in(key, 6)
    for dim, blocks in pieces:
        steps = jnp.exp(jax.random.uniform(jax.random.fold_in(own, dim), (blocks,), jnp.float32, low / len(pieces), largest / len(pieces)))
        gain = gain * jnp.repeat(steps, shape[dim] // blocks).reshape([-1 if axis == dim else 1 for axis in range(len(shape))])
    return gain


def shared_out(stream_key, own, number, rows, count, top, most, skew):
    ranking = jax.random.permutation(stream_key, count)
    packed, ordinary = shares(count, rows * top, most, skew, True), shares(count, rows * top, most, skew, False)
    places = jnp.arange(count)

    def named(tallies, turn):
        used = int((tallies > 0).sum())
        fixed = max(1, used // 4)
        shifted = fixed + (places - fixed + turn * (used - fixed)) % max(1, count - fixed)
        return jnp.zeros((count,), jnp.int32).at[ranking[jnp.where(places < fixed, places, shifted)]].set(jnp.asarray(tallies, jnp.int32))

    tallies = jnp.where(number % 4 == 0, named(packed, number // 4), named(ordinary, number - number // 4 - 1))
    mixed = jax.random.permutation(jax.random.fold_in(own, 3), count)
    giver, receiver = mixed[0:count // 2 * 2:2], mixed[1:count // 2 * 2:2]
    room = jnp.minimum(tallies[giver] - 1, most - tallies[receiver]) // 2
    room = jnp.where((giver == ranking[0]) | (receiver == ranking[0]) | (tallies[receiver] == 0), 0, jnp.maximum(room, 0))
    shifted = jax.random.randint(jax.random.fold_in(own, 4), (count // 2,), 0, 1 << 20) % (room + 1)
    tallies = tallies.at[giver].add(-shifted).at[receiver].add(shifted)
    items = jnp.searchsorted(jnp.cumsum(tallies), jnp.arange(rows * top), side="right").astype(jnp.int32)
    grid = items.reshape(top, rows).T
    grid = grid[jax.random.permutation(jax.random.fold_in(own, 1), rows)]
    turn = jax.random.randint(jax.random.fold_in(own, 2), (rows, 1), 0, top)
    return jnp.take_along_axis(grid, (jnp.arange(top)[None, :] + turn) % top, axis=1)


def shares(count, total, limit, lean, full):
    portions = [(1 << 20) // math.isqrt(standing ** lean) + 1 for standing in range(1, count + 1)]
    largest = limit if full else min(limit, max(-(-total // count), total * portions[0] // sum(portions)))
    least = 1 if total - largest >= count - 1 else 0
    counts, spare = [largest] + [least] * (count - 1), total - largest - least * (count - 1)
    while spare > 0:
        free = [i for i in range(1, count) if counts[i] < largest] or [i for i in range(1, count) if counts[i] < limit]
        pool, budget = sum([portions[i] for i in free]), spare
        for i in free:
            more = min(limit - counts[i], max(1, budget * portions[i] // pool), spare)
            counts[i] = counts[i] + more
            spare = spare - more
    return np.array(counts)


def normal_values(own_key, dims, spread, reach, cuts=(), kind=jnp.bfloat16):
    result = jax.random.normal(own_key, dims, jnp.float32) * spread
    if len(cuts) > 0:
        result = block_scale(own_key, dims, cuts, -0.22, 0.18) * result
    return jnp.clip(result, min=-reach, max=reach).astype(kind)


def setup_inputs(seed: int = 0) -> dict:
    splits = jax.random.split(jax.random.key(seed), 7)
    positions = normal_values(splits[0], (CELLS, 3, P_SIZE), 1.0, 6.0, ((0, 32),), jnp.float32)
    analysis = normal_values(splits[1], (NCOEF, P_SIZE), P_SIZE ** -0.5, 0.25, (), jnp.float32)
    synthesis = normal_values(splits[2], (P_SIZE, NCOEF), NCOEF ** -0.5, 0.375, (), jnp.float32)
    stiffness = jnp.clip(jnp.exp(jax.random.uniform(splits[3], (NCOEF,), jnp.float32, math.log(0.1), math.log(10.0))), 0.1, 10.0)
    owner_keys = jax.random.split(jax.random.fold_in(splits[4], 1), NBLK // BLK_DEV)
    owner_turns = jax.random.permutation(jax.random.fold_in(splits[4], 3), NBLK // BLK_DEV)
    owner = jax.vmap(lambda own, number: shared_out(jax.random.fold_in(splits[4], 2), own, number, BLK_DEV, N_DEV, 1, CAP, 2))(owner_keys, owner_turns).reshape((NBLK, 1))
    ulist = draw_ulist(jax.random.fold_in(splits[6], 71), 0)
    return {"positions": positions, "analysis": analysis, "synthesis": synthesis, "stiffness": stiffness, "owner": owner, "ulist": ulist}


SOFTENING = 0.25
KERNEL = 1.0 / (8.0 * math.pi)
TIME_STEP = 0.02
PRECISE = lax.Precision.HIGHEST

def spectral(shape_field, analysis, synthesis, weights):
    coeffs = jnp.einsum('ckp,mp->ckm', shape_field, analysis, precision=PRECISE)
    return jnp.einsum('ckm,pm->ckp', coeffs * weights, synthesis, precision=PRECISE)

def stokeslet(targets, sources):
    offset = targets[:, :, :, None] - sources[:, 0:3, None, :]
    forces = sources[:, 3:6, None, :]
    dist_sq = lax.optimization_barrier(jnp.sum(offset * offset, axis=1)) + SOFTENING
    kernel_scale = KERNEL / (dist_sq * jnp.sqrt(dist_sq))
    projected = lax.optimization_barrier(jnp.sum(offset * forces, axis=1))
    summed = ((dist_sq + SOFTENING) * kernel_scale)[:, None] * forces + (projected * kernel_scale)[:, None] * offset
    return lax.optimization_barrier(jnp.sum(summed, axis=3))

def reference(positions, analysis, synthesis, stiffness, owner, ulist):
    groups = N_GROUP
    dev_count = N_DEV
    device_count = groups * dev_count
    capacity = CAP
    slot_count = SLOTS
    block_count = device_count * BLK_DEV
    owner_dev = owner[:, 0].reshape(device_count, BLK_DEV)
    same_owner = owner_dev[:, :, None] == owner_dev[:, None, :]
    order_idx = jnp.arange(BLK_DEV, dtype=jnp.int32)
    earlier = order_idx[None, :] < order_idx[:, None]
    block_rank = lax.optimization_barrier(jnp.sum(jnp.where(same_owner & earlier[None], 1, 0), axis=2)).astype(jnp.int32)
    dev_all = jnp.arange(device_count, dtype=jnp.int32)
    group_of = dev_all // dev_count
    source_dev = dev_all % dev_count
    recv_dev = group_of[:, None] * dev_count + owner_dev
    recv_slot = source_dev[:, None] * capacity + block_rank
    flat_row = (recv_dev * slot_count + recv_slot).reshape(-1).astype(jnp.int32)
    slot_table = jnp.full((device_count * slot_count,), block_count, jnp.int32)
    slot_table = slot_table.at[flat_row].set(jnp.arange(block_count, dtype=jnp.int32))
    entries = ulist[flat_row]
    group_side = entries // slot_count
    slot_pos = entries % slot_count
    source_group = jnp.repeat(group_of, BLK_DEV)[:, None] + group_side - 1
    usable = (source_group >= 0) & (source_group < groups)
    owner_flat = owner_dev.reshape(-1)[:, None]
    lookup = ((jnp.clip(source_group, 0, groups - 1) * dev_count + owner_flat) * slot_count + slot_pos).astype(jnp.int32)
    source_ids = jnp.where(usable, slot_table[lookup], block_count).astype(jnp.int32)

    def to_blocks(values):
        shaped = values.reshape(device_count, C_DEV, 3, P_SIZE).transpose(0, 2, 1, 3)
        shaped = shaped.reshape(device_count, 3, BLK_DEV, LEAF).transpose(0, 2, 1, 3)
        return shaped.reshape(block_count, 3, LEAF)

    def from_blocks(values):
        shaped = values.reshape(device_count, BLK_DEV, 3, LEAF).transpose(0, 2, 1, 3)
        shaped = shaped.reshape(device_count, 3, C_DEV, P_SIZE).transpose(0, 2, 1, 3)
        return shaped.reshape(device_count * C_DEV, 3, P_SIZE)
    ones = jnp.ones((NCOEF,), jnp.float32)
    shape_field = positions
    velocity = jnp.zeros_like(positions)
    for time_step in range(STEPS):
        forces = -spectral(shape_field, analysis, synthesis, stiffness)
        payload = jnp.concatenate([to_blocks(shape_field), to_blocks(forces)], axis=1)
        payload = jnp.concatenate([payload, jnp.zeros((1, 6, LEAF), jnp.float32)], axis=0)

        def per_batch(block_ids):
            targets = payload[block_ids, 0:3]
            summed = jnp.zeros((block_ids.shape[0], 3, LEAF), jnp.float32)
            for entry in range(KNEAR):
                summed = summed + stokeslet(targets, payload[source_ids[block_ids, entry]])
            return summed
        flows = lax.map(per_batch, jnp.arange(block_count, dtype=jnp.int32).reshape(-1, 32))
        velocity = from_blocks(flows.reshape(block_count, 3, LEAF))
        shape_field = spectral(shape_field + TIME_STEP * velocity, analysis, synthesis, ones)
    return (shape_field, velocity)
```

```python
import functools
import math

import jax
import jax.numpy as jnp
from jax import lax
from jax.experimental import pallas as pl
from jax.experimental.pallas import tpu as pltpu
from jax.sharding import PartitionSpec as P

LEAF = 128
ROWS = 16
SOFTENING = 0.25
ROOT = math.sqrt(SOFTENING)
KERNEL = 1.0 / (8.0 * math.pi)
TIME_STEP = 0.02
MESH = pl.DeviceIdType.MESH
BF16, F32 = jnp.bfloat16, jnp.float32


def split3(value):
    first = value.astype(BF16)
    rest = value - first.astype(F32)
    second = rest.astype(BF16)
    third = (rest - second.astype(F32)).astype(BF16)
    return first, second, third


def split2(value):
    first = value.astype(BF16)
    return first, (value - first.astype(F32)).astype(BF16)


def product(left, right_high, right_low, dims):
    high, low = split2(left)
    dot = functools.partial(
        lax.dot_general, dimension_numbers=(dims, ((), ())), preferred_element_type=F32
    )
    return dot(high, right_high) + (dot(low, right_high) + dot(high, right_low))


def beside(group, groups, action):
    pl.when(group + 1 < groups)(functools.partial(action, 0, group + 1))
    pl.when(group > 0)(functools.partial(action, 1, group - 1))


def kernel(
    capacity, knear,
    lists_ref, pos_hbm, ana_hbm, syn_hbm, stiff_hbm, owner_hbm,
    moved_ref, vel_ref,
    pos_ref, ana_ref, syn_ref, stiff_ref, owner_ref,
    ana_high, ana_low, syn_high, syn_low,
    packed_ref, near_ref, table_ref, target_ref, flows_ref, back_ref,
    dist0_ref, dist1_ref, value0_ref, value1_ref,
    load_sem, own_sem, send_sem, recv_sem, side_send, side_recv, back_send, back_recv,
):
    count, groups = lax.axis_size("dev"), lax.axis_size("group")
    me, group = lax.axis_index("dev"), lax.axis_index("group")
    slots = count * capacity
    rows, points = pos_ref.shape
    cells = rows // 3
    blocks = owner_ref.shape[1]
    tiles = pl.cdiv(points, LEAF)
    padded = tiles + tiles % 2

    barrier = pltpu.get_barrier_semaphore()

    def signal(step, carry):
        pl.semaphore_signal(
            barrier, inc=1, device_id={"dev": lax.rem(me + step, count)}, device_id_type=MESH
        )
        return carry

    lax.fori_loop(1, count, signal, 0)
    beside(
        group, groups,
        lambda way, other: pl.semaphore_signal(
            barrier, inc=1, device_id={"group": other}, device_id_type=MESH
        ),
    )
    loads = [
        pltpu.make_async_copy(src, dst, load_sem.at[number])
        for number, (src, dst) in enumerate(
            [
                (owner_hbm, owner_ref), (pos_hbm, pos_ref), (ana_hbm, ana_ref),
                (syn_hbm, syn_ref), (stiff_hbm, stiff_ref),
            ]
        )
    ]
    for load in loads:
        load.start()

    value1_ref[...] = jnp.zeros_like(value1_ref)

    loads[0].wait()
    piece = lax.broadcasted_iota(jnp.int32, (padded * cells, 1), 0)
    block = (piece % cells) * points // LEAF + piece // cells
    lane_block = lax.broadcasted_iota(jnp.int32, (padded * cells, blocks), 1)
    owner_row = owner_ref[...].astype(F32)
    owner_col = jnp.sum(jnp.where(block == lane_block, owner_row, 0.0), axis=1, keepdims=True)
    earlier = (owner_row == owner_col) & (lane_block < block)
    rank_col = jnp.sum(jnp.where(earlier, 1.0, 0.0), axis=1, keepdims=True)
    place = (rank_col * count + owner_col).astype(jnp.int32)
    place = jnp.where(piece < tiles * cells, place, slots)
    take = place == lax.broadcasted_iota(jnp.int32, (padded * cells, slots), 1)
    take = jnp.where(take, 1.0, 0.0)
    give = take.T.astype(BF16)
    take = take.astype(BF16)

    lane = lax.broadcasted_iota(jnp.int32, (rows, LEAF), 1)
    shift = points % LEAF
    cell = lax.broadcasted_iota(jnp.int32, (rows, LEAF), 0) % cells
    start = cell * shift % LEAF

    def turn(value, way):
        for bit in range((cells - 1).bit_length()):
            amount = way * (shift << bit) % LEAF
            if amount:
                rolled = pltpu.roll(value, amount, 1)
                value = jnp.where(cell // (1 << bit) % 2 == 1, rolled, value)
        return value

    def to_pieces(value):
        pieces, before = [], jnp.zeros((rows, LEAF), F32)
        for tile in range(tiles):
            part = value[:, tile * LEAF : min((tile + 1) * LEAF, points)]
            if part.shape[1] < LEAF:
                blank = jnp.zeros((rows, LEAF - part.shape[1]), F32)
                part = jnp.concatenate([part, blank], axis=1)
            part = turn(part, 1)
            pieces.append(jnp.where(lane >= start, part, before))
            before = part
        pieces += [jnp.zeros((rows, LEAF), F32)] * (padded - tiles)
        return [
            jnp.concatenate([p[k * cells : (k + 1) * cells] for p in pieces], axis=0)
            for k in range(3)
        ]

    def pack(value, first):
        pieces = split3(jnp.concatenate(to_pieces(value), axis=1))
        sent = sum(jnp.dot(give, piece, preferred_element_type=F32) for piece in pieces)
        for k in range(3):
            for r in range(capacity):
                packed_ref[:, (first + k) * capacity + r, :] = sent[
                    r * count : (r + 1) * count, k * LEAF : (k + 1) * LEAF
                ]

    loads[1].wait()
    field = pos_ref[...]
    pack(field, 0)
    loads[2].wait()
    ana_high[...], ana_low[...] = split2(ana_ref[...])
    loads[3].wait()
    syn_high[...], syn_low[...] = split2(syn_ref[...])
    loads[4].wait()
    coeffs = product(field, ana_high[...], ana_low[...], ((1,), (1,)))
    forces = -product(coeffs * stiff_ref[...], syn_high[...], syn_low[...], ((1,), (0,)))
    pack(forces, 3)

    sides = jnp.minimum(group, 1) + jnp.minimum(groups - 1 - group, 1)
    pl.semaphore_wait(barrier, count - 1 + sides)

    def step_of(number):
        half = (number + 1) // 2
        sign = 2 * (number % 2) - 1
        return count // 2 + sign * half

    def across(step):
        peer = lax.rem(me + step, count)
        return pltpu.make_async_remote_copy(
            src_ref=packed_ref.at[peer],
            dst_ref=near_ref.at[1, me],
            send_sem=send_sem.at[step],
            recv_sem=recv_sem.at[step],
            device_id={"dev": peer},
            device_id_type=MESH,
        )

    def along(step, way, other):
        chunk = lax.rem(me - step + count, count)
        return pltpu.make_async_remote_copy(
            src_ref=near_ref.at[1, chunk],
            dst_ref=near_ref.at[2 * way, chunk],
            send_sem=side_send.at[way, step],
            recv_sem=side_recv.at[way, step],
            device_id={"group": other},
            device_id_type=MESH,
        )

    def across_back(step):
        home = lax.rem(me - step + count, count)
        return pltpu.make_async_remote_copy(
            src_ref=flows_ref.at[home],
            dst_ref=back_ref.at[me],
            send_sem=back_send.at[step],
            recv_sem=back_recv.at[step],
            device_id={"dev": home},
            device_id_type=MESH,
        )

    own = pltpu.make_async_copy(packed_ref.at[me], near_ref.at[1, me], own_sem)
    own.start()

    def send(number, carry):
        across(step_of(number)).start()
        return carry

    lax.fori_loop(0, count - 1, send, 0)

    def prepare(data, slot):
        y, f = data[0:3], data[3:6]
        ones = jnp.ones((1, LEAF), F32)
        zeros3, zeros4 = jnp.zeros((3, LEAF), F32), jnp.zeros((4, LEAF), F32)
        y_sq = jnp.sum(y * y, axis=0, keepdims=True)
        yf = -jnp.sum(y * f, axis=0, keepdims=True)
        scale = 1.0 / SOFTENING
        dist = jnp.concatenate(
            [(-2.0 * scale) * y, scale * y_sq + 1.0, scale * ones, zeros3], axis=0
        )
        proj = jnp.concatenate([f, yf, zeros4], axis=0)
        d1, d2, d3 = [part.astype(F32) for part in split3(dist)]
        p1, p2, p3 = [part.astype(F32) for part in split3(proj)]
        w_f = jnp.concatenate([f * (KERNEL / ROOT), jnp.zeros((5, LEAF), F32)], axis=0)
        cube = KERNEL / ROOT**3
        w_y = jnp.concatenate([-cube * y, cube * ones, zeros4], axis=0)
        f1, f2 = [part.astype(F32) for part in split2(w_f)]
        y1, y2 = [part.astype(F32) for part in split2(w_y)]
        left = jnp.concatenate([d1, d2, d3, d1, d2, d1, f1, f2], axis=0)
        right = jnp.concatenate([p1, p2, p3, p1, p2, p1, y1, y2], axis=0)
        table_ref[slot, :, 0:LEAF] = left.astype(BF16)
        table_ref[slot, :, LEAF:] = right.astype(BF16)
        return y, y_sq

    def prepare_target(x, x_sq, slot):
        ones = jnp.ones((1, LEAF), F32)
        base = jnp.concatenate([x, ones, x_sq, jnp.zeros((3, LEAF), F32)], axis=0)
        t1, t2, t3 = [part.astype(F32) for part in split3(base)]
        target = jnp.concatenate([t1, t1, t1, t2, t2, t3], axis=0)
        target_ref[slot] = target.T.astype(BF16)

    def slot_data(side, home, r):
        return near_ref[side, home, pl.ds(r, 6, stride=capacity), :]

    def arrived(home):
        for r in range(capacity):
            slot = home * capacity + r
            x, x_sq = prepare(slot_data(1, home, r), slots + slot)
            prepare_target(x, x_sq, slot)

    prepare(jnp.zeros((6, LEAF), F32), 3 * slots)
    own.wait()
    beside(group, groups, lambda way, other: along(0, way, other).start())
    arrived(me)

    def relay(number, carry):
        step = step_of(number)
        across(step).wait_recv()
        beside(group, groups, lambda way, other: along(step, way, other).start())
        arrived(lax.rem(me - step + count, count))
        return carry

    lax.fori_loop(0, count - 1, relay, 0)

    def side_arrived(step):
        chunk = lax.rem(me - step + count, count)

        def accept(way, other):
            along(step, way, other).wait_recv()
            for r in range(capacity):
                slot = 2 * way * slots + chunk * capacity + r
                prepare(slot_data(2 * way, chunk, r), slot)

        pl.when(group > 0)(lambda: accept(0, group - 1))
        pl.when(group + 1 < groups)(lambda: accept(1, group + 1))

    side_arrived(0)

    def side_relay(number, carry):
        side_arrived(step_of(number))
        return carry

    lax.fori_loop(0, count - 1, side_relay, 0)

    low = jnp.where(group == 0, slots, 0)
    high = jnp.where(group == groups - 1, 2 * slots, 3 * slots)

    def source(slot, entry):
        named = lists_ref[entry, slot]
        return jnp.where((named >= low) & (named < high), named, 3 * slots)

    def distances(slot, out_ref):
        for entry in range(knear):
            out_ref[entry] = jnp.dot(
                target_ref[slot],
                table_ref[source(slot, entry), 0:48],
                preferred_element_type=F32,
            )

    def kernels(in_ref, out_ref):
        for entry in range(knear):
            for row in range(0, LEAF, ROWS):
                rr = in_ref[entry, row : row + ROWS, 0:LEAF]
                projected = in_ref[entry, row : row + ROWS, LEAF:]
                inv = lax.rsqrt(rr)
                inv3 = inv * inv * inv
                parts = split2(inv + inv3) + split2(projected * inv3)
                for part in range(4):
                    at = (4 * entry + part) * LEAF
                    out_ref[row : row + ROWS, at : at + LEAF] = parts[part]

    def sums(home, r, in_ref, keep):
        slot = home * capacity + r
        weights = []
        for entry in range(knear):
            number = source(slot, entry)
            w_f = table_ref[number, 48:64, 0:LEAF]
            w_y = table_ref[number, 48:64, LEAF:]
            weights += [w_f, w_f, w_y, w_y]
        part = lax.dot_general(
            jnp.concatenate(weights, axis=1),
            in_ref[...],
            (((1,), (1,)), ((), ())),
            preferred_element_type=F32,
        )
        total = part[0:8] + part[8:16]
        x = near_ref[1, home, pl.ds(r, 3, stride=capacity), :]
        flows_ref[keep, pl.ds(r, 3, stride=capacity), :] = total[0:3] + x * total[3:4]

    def home_of(number):
        step = jnp.where(number < count - 1, step_of(number), 0)
        return lax.rem(me - step + count, count)

    dist = (dist0_ref, dist1_ref)
    value = (value0_ref, value1_ref)
    distances(home_of(0) * capacity, dist0_ref)

    def chunk(number, carry):
        home = home_of(number)
        after = home_of(jnp.minimum(number + 1, count - 1))
        last = jnp.maximum(number - 1, 0)
        before = home_of(last)
        for r in range(capacity):
            parity = r % 2
            following = home * capacity + r + 1 if r + 1 < capacity else after * capacity
            distances(following, dist[1 - parity])
            kernels(dist[parity], value[parity])
            if r:
                sums(home, r - 1, value[1 - parity], home)
            else:
                keep = jnp.where(number > 0, before, count)
                sums(before, capacity - 1, value[1 - parity], keep)

        @pl.when(number > 0)
        def _():
            across_back(step_of(last)).start()

        return carry

    lax.fori_loop(0, count, chunk, 0)
    sums(me, capacity - 1, value1_ref, me)
    back_ref[me] = flows_ref[me]

    def finish(number, carry):
        across_back(step_of(number)).wait_recv()
        return carry

    lax.fori_loop(0, count - 1, finish, 0)

    returned = [
        jnp.concatenate([back_ref[:, k * capacity + r, :] for r in range(capacity)], axis=0)
        for k in range(3)
    ]
    pieces = split3(jnp.concatenate(returned, axis=1))
    taken = sum(jnp.dot(take, piece, preferred_element_type=F32) for piece in pieces)
    tile_rows = [
        jnp.concatenate(
            [
                taken[t * cells : (t + 1) * cells, k * LEAF : (k + 1) * LEAF]
                for k in range(3)
            ],
            axis=0,
        )
        for t in range(tiles)
    ]
    for tile in range(tiles):
        part = tile_rows[tile]
        if tile + 1 < tiles:
            part = jnp.where(lane >= start, part, tile_rows[tile + 1])
        part = turn(part, -1)
        width = min(LEAF, points - tile * LEAF)
        vel_ref[:, tile * LEAF : tile * LEAF + width] = part[:, 0:width]
    stepped = pos_ref[...] + TIME_STEP * vel_ref[...]
    coeffs = product(stepped, ana_high[...], ana_low[...], ((1,), (1,)))
    moved_ref[...] = product(coeffs, syn_high[...], syn_low[...], ((1,), (0,)))

    def sent(number, carry):
        step = step_of(number)
        across(step).wait_send()
        across_back(step).wait_send()
        return carry

    lax.fori_loop(0, count - 1, sent, 0)

    def side_sent(step, carry):
        beside(group, groups, lambda way, other: along(step, way, other).wait_send())
        return carry

    lax.fori_loop(0, count, side_sent, 0)


def shards(positions, analysis, synthesis, stiffness, owner, ulist):
    count = lax.axis_size("dev")
    cells, dims, points = positions.shape
    coefs = analysis.shape[0]
    blocks = owner.shape[0]
    knear = ulist.shape[1]
    capacity = ulist.shape[0] // count
    slots = count * capacity
    rows = dims * cells
    sem = pltpu.SemaphoreType.DMA
    shape = jax.ShapeDtypeStruct((rows, points), F32)
    any_spec = pl.BlockSpec(memory_space=pl.ANY)
    vmem_spec = pl.BlockSpec(memory_space=pltpu.VMEM)
    moved, velocity = pl.pallas_call(
        functools.partial(kernel, capacity, knear),
        out_shape=(shape, shape),
        in_specs=[pl.BlockSpec(memory_space=pltpu.SMEM)] + [any_spec] * 5,
        out_specs=(vmem_spec, vmem_spec),
        scratch_shapes=[
            pltpu.VMEM((rows, points), F32),
            pltpu.VMEM((coefs, points), F32),
            pltpu.VMEM((coefs, points), F32),
            pltpu.VMEM((1, coefs), F32),
            pltpu.VMEM((1, blocks), jnp.int32),
            pltpu.VMEM((coefs, points), BF16),
            pltpu.VMEM((coefs, points), BF16),
            pltpu.VMEM((coefs, points), BF16),
            pltpu.VMEM((coefs, points), BF16),
            pltpu.VMEM((count, 6 * capacity, LEAF), F32),
            pltpu.VMEM((3, count, 6 * capacity, LEAF), F32),
            pltpu.VMEM((3 * slots + 1, 64, 2 * LEAF), BF16),
            pltpu.VMEM((slots, LEAF, 48), BF16),
            pltpu.VMEM((count + 1, 3 * capacity, LEAF), F32),
            pltpu.VMEM((count, 3 * capacity, LEAF), F32),
            pltpu.VMEM((knear, LEAF, 2 * LEAF), F32),
            pltpu.VMEM((knear, LEAF, 2 * LEAF), F32),
            pltpu.VMEM((LEAF, 4 * knear * LEAF), BF16),
            pltpu.VMEM((LEAF, 4 * knear * LEAF), BF16),
            sem((5,)), sem, sem((count,)), sem((count,)), sem((2, count)), sem((2, count)),
            sem((count,)), sem((count,)),
        ],
        compiler_params=pltpu.CompilerParams(collective_id=0, has_side_effects=True),
    )(
        ulist.T,
        positions.transpose(1, 0, 2).reshape(rows, points),
        analysis,
        synthesis.T,
        stiffness.reshape(1, coefs),
        owner.reshape(1, blocks),
    )

    def to_cells(value):
        return value.reshape(dims, cells, points).transpose(1, 0, 2)

    return to_cells(moved), to_cells(velocity)


def solution(mesh):
    placed = (
        P(("group", "dev"), None, None),
        P(),
        P(),
        P(),
        P(("group", "dev"), None),
        P(("group", "dev"), None),
    )
    return jax.shard_map(
        shards,
        mesh=mesh,
        in_specs=placed,
        out_specs=(P(("group", "dev"), None, None), P(("group", "dev"), None, None)),
        check_vma=False,
    )
```

```python
import functools
import math

import jax
import jax.numpy as jnp
from jax import lax
from jax.experimental import pallas as pl
from jax.experimental.pallas import tpu as pltpu
from jax.sharding import PartitionSpec as P

LEAF = 128
ROWS = 16
SOFTENING = 0.25
ROOT = math.sqrt(SOFTENING)
KERNEL = 1.0 / (8.0 * math.pi)
TIME_STEP = 0.02
MESH = pl.DeviceIdType.MESH
BF16, F32 = jnp.bfloat16, jnp.float32


def split3(value):
    first = value.astype(BF16)
    rest = value - first.astype(F32)
    second = rest.astype(BF16)
    third = (rest - second.astype(F32)).astype(BF16)
    return first, second, third


def split2(value):
    first = value.astype(BF16)
    return first, (value - first.astype(F32)).astype(BF16)


def product(left, right_high, right_low, dims):
    high, low = split2(left)
    dot = functools.partial(
        lax.dot_general, dimension_numbers=(dims, ((), ())), preferred_element_type=F32
    )
    return dot(high, right_high) + (dot(low, right_high) + dot(high, right_low))


def beside(group, groups, action):
    pl.when(group + 1 < groups)(functools.partial(action, 0, group + 1))
    pl.when(group > 0)(functools.partial(action, 1, group - 1))


def kernel(
    capacity, knear,
    lists_hbm, pos_hbm, ana_hbm, syn_hbm, stiff_hbm, owner_hbm,
    moved_ref, vel_ref,
    lists_ref, pos_ref, ana_ref, syn_ref, stiff_ref, owner_ref,
    ana_high, ana_low, syn_high, syn_low,
    packed_ref, near_ref, table_ref, target_ref, flows_ref, back_ref,
    self_dist, self_value, partial_ref, *rest,
):
    dist, value, rest = rest[:capacity], rest[capacity : 2 * capacity], rest[2 * capacity :]
    load_sem, own_sem, send_sem, recv_sem, side_send, side_recv, back_send, back_recv = rest
    count, groups = lax.axis_size("dev"), lax.axis_size("group")
    me, group = lax.axis_index("dev"), lax.axis_index("group")
    slots = count * capacity
    rows, points = pos_ref.shape
    cells = rows // 3
    blocks = owner_ref.shape[1]
    tiles = pl.cdiv(points, LEAF)
    padded = tiles + tiles % 2

    barrier = pltpu.get_barrier_semaphore()

    def signal(step, carry):
        pl.semaphore_signal(
            barrier, inc=1, device_id={"dev": lax.rem(me + step, count)}, device_id_type=MESH
        )
        return carry

    lax.fori_loop(1, count, signal, 0)
    beside(
        group, groups,
        lambda way, other: pl.semaphore_signal(
            barrier, inc=1, device_id={"group": other}, device_id_type=MESH
        ),
    )
    loads = [
        pltpu.make_async_copy(src, dst, load_sem.at[number])
        for number, (src, dst) in enumerate(
            [
                (owner_hbm, owner_ref), (pos_hbm, pos_ref), (ana_hbm, ana_ref),
                (syn_hbm, syn_ref), (stiff_hbm, stiff_ref),
                (lists_hbm, lists_ref),
            ]
        )
    ]
    for load in loads:
        load.start()

    self_value[...] = jnp.zeros_like(self_value)
    for ref in value:
        ref[...] = jnp.zeros_like(ref)

    loads[0].wait()
    piece = lax.broadcasted_iota(jnp.int32, (padded * cells, 1), 0)
    block = (piece % cells) * points // LEAF + piece // cells
    lane_block = lax.broadcasted_iota(jnp.int32, (padded * cells, blocks), 1)
    owner_row = owner_ref[...].astype(F32)
    owner_col = jnp.sum(jnp.where(block == lane_block, owner_row, 0.0), axis=1, keepdims=True)
    earlier = (owner_row == owner_col) & (lane_block < block)
    rank_col = jnp.sum(jnp.where(earlier, 1.0, 0.0), axis=1, keepdims=True)
    place = (rank_col * count + owner_col).astype(jnp.int32)
    place = jnp.where(piece < tiles * cells, place, slots)
    take = place == lax.broadcasted_iota(jnp.int32, (padded * cells, slots), 1)
    take = jnp.where(take, 1.0, 0.0)
    give = take.T.astype(BF16)
    take = take.astype(BF16)

    lane = lax.broadcasted_iota(jnp.int32, (rows, LEAF), 1)
    shift = points % LEAF
    cell = lax.broadcasted_iota(jnp.int32, (rows, LEAF), 0) % cells
    start = cell * shift % LEAF

    def turn(value, way):
        for bit in range((cells - 1).bit_length()):
            amount = way * (shift << bit) % LEAF
            if amount:
                rolled = pltpu.roll(value, amount, 1)
                value = jnp.where(cell // (1 << bit) % 2 == 1, rolled, value)
        return value

    def to_pieces(value):
        pieces, before = [], jnp.zeros((rows, LEAF), F32)
        for tile in range(tiles):
            part = value[:, tile * LEAF : min((tile + 1) * LEAF, points)]
            if part.shape[1] < LEAF:
                blank = jnp.zeros((rows, LEAF - part.shape[1]), F32)
                part = jnp.concatenate([part, blank], axis=1)
            part = turn(part, 1)
            pieces.append(jnp.where(lane >= start, part, before))
            before = part
        pieces += [jnp.zeros((rows, LEAF), F32)] * (padded - tiles)
        return [
            jnp.concatenate([p[k * cells : (k + 1) * cells] for p in pieces], axis=0)
            for k in range(3)
        ]

    def pack(value, first):
        pieces = split3(jnp.concatenate(to_pieces(value), axis=1))
        sent = sum(jnp.dot(give, piece, preferred_element_type=F32) for piece in pieces)
        for k in range(3):
            for r in range(capacity):
                packed_ref[:, (first + k) * capacity + r, :] = sent[
                    r * count : (r + 1) * count, k * LEAF : (k + 1) * LEAF
                ]

    loads[1].wait()
    field = pos_ref[...]
    pack(field, 0)
    loads[2].wait()
    ana_high[...], ana_low[...] = split2(ana_ref[...])
    loads[3].wait()
    syn_high[...], syn_low[...] = split2(syn_ref[...])
    loads[4].wait()
    coeffs = product(field, ana_high[...], ana_low[...], ((1,), (1,)))
    forces = -product(coeffs * stiff_ref[...][None, :], syn_high[...], syn_low[...], ((1,), (0,)))
    pack(forces, 3)

    sides = jnp.minimum(group, 1) + jnp.minimum(groups - 1 - group, 1)
    pl.semaphore_wait(barrier, count - 1 + sides)

    def step_of(number):
        half = (number + 1) // 2
        sign = 2 * (number % 2) - 1
        return count // 2 + sign * half

    def across(step):
        peer = lax.rem(me + step, count)
        return pltpu.make_async_remote_copy(
            src_ref=packed_ref.at[peer],
            dst_ref=near_ref.at[1, me],
            send_sem=send_sem.at[step],
            recv_sem=recv_sem.at[step],
            device_id={"dev": peer},
            device_id_type=MESH,
        )

    def along(step, way, other):
        chunk = lax.rem(me - step + count, count)
        return pltpu.make_async_remote_copy(
            src_ref=near_ref.at[1, chunk],
            dst_ref=near_ref.at[2 * way, chunk],
            send_sem=side_send.at[way, step],
            recv_sem=side_recv.at[way, step],
            device_id={"group": other},
            device_id_type=MESH,
        )

    def across_back(step):
        home = lax.rem(me - step + count, count)
        return pltpu.make_async_remote_copy(
            src_ref=flows_ref.at[home],
            dst_ref=back_ref.at[me],
            send_sem=back_send.at[step],
            recv_sem=back_recv.at[step],
            device_id={"dev": home},
            device_id_type=MESH,
        )

    own = pltpu.make_async_copy(packed_ref.at[me], near_ref.at[1, me], own_sem)
    own.start()

    def send(number, carry):
        across(step_of(number)).start()
        return carry

    lax.fori_loop(0, count - 1, send, 0)

    def prepare(data, slot):
        y, f = data[0:3], data[3:6]
        ones = jnp.ones((1, LEAF), F32)
        zeros3, zeros4 = jnp.zeros((3, LEAF), F32), jnp.zeros((4, LEAF), F32)
        y_sq = jnp.sum(y * y, axis=0, keepdims=True)
        yf = -jnp.sum(y * f, axis=0, keepdims=True)
        scale = 1.0 / SOFTENING
        dist = jnp.concatenate(
            [(-2.0 * scale) * y, scale * y_sq + 1.0, scale * ones, zeros3], axis=0
        )
        proj = jnp.concatenate([f, yf, zeros4], axis=0)
        d1, d2, d3 = [part.astype(F32) for part in split3(dist)]
        p1, p2, p3 = [part.astype(F32) for part in split3(proj)]
        w_f = jnp.concatenate([f * (KERNEL / ROOT), jnp.zeros((5, LEAF), F32)], axis=0)
        cube = KERNEL / ROOT**3
        w_y = jnp.concatenate([-cube * y, cube * ones, zeros4], axis=0)
        f1, f2 = [part.astype(F32) for part in split2(w_f)]
        y1, y2 = [part.astype(F32) for part in split2(w_y)]
        left = jnp.concatenate([d1, d2, d3, d1, d2, d1, f1, f2], axis=0)
        right = jnp.concatenate([p1, p2, p3, p1, p2, p1, y1, y2], axis=0)
        table_ref[slot, :, 0:LEAF] = left.astype(BF16)
        table_ref[slot, :, LEAF:] = right.astype(BF16)
        return y, y_sq

    def prepare_target(x, x_sq, slot):
        ones = jnp.ones((1, LEAF), F32)
        base = jnp.concatenate([x, ones, x_sq, jnp.zeros((3, LEAF), F32)], axis=0)
        t1, t2, t3 = [part.astype(F32) for part in split3(base)]
        target = jnp.concatenate([t1, t1, t1, t2, t2, t3], axis=0)
        target_ref[slot] = target.T.astype(BF16)

    def slot_data(side, home, r):
        return near_ref[side, home, pl.ds(r, 6, stride=capacity), :]

    def arrived(home):
        for r in range(capacity):
            slot = home * capacity + r
            x, x_sq = prepare(slot_data(1, home, r), slots + slot)
            prepare_target(x, x_sq, slot)

    def distances(slot, number):
        return jnp.dot(target_ref[slot], table_ref[number, 0:48], preferred_element_type=F32)

    def kernels(items, in_ref, out_ref):
        for item in range(items):
            for row in range(0, LEAF, ROWS):
                rr = in_ref[item, row : row + ROWS, 0:LEAF]
                projected = in_ref[item, row : row + ROWS, LEAF:]
                inv = lax.rsqrt(rr)
                inv3 = inv * inv * inv
                parts = split2(inv + inv3) + split2(projected * inv3)
                for part in range(4):
                    at = (4 * item + part) * LEAF
                    out_ref[row : row + ROWS, at : at + LEAF] = parts[part]

    def sums(numbers, values):
        weights = []
        for number in numbers:
            w_f = table_ref[number, 48:64, 0:LEAF]
            w_y = table_ref[number, 48:64, LEAF:]
            weights += [w_f, w_f, w_y, w_y]
        part = lax.dot_general(
            jnp.concatenate(weights, axis=1),
            values,
            (((1,), (1,)), ((), ())),
            preferred_element_type=F32,
        )
        return part[0:8] + part[8:16]

    def self_distances(home):
        for r in range(capacity):
            slot = home * capacity + r
            self_dist[r] = distances(slot, slots + slot)

    def self_sums(home, keep):
        for r in range(capacity):
            values = self_value[:, 4 * r * LEAF : 4 * (r + 1) * LEAF]
            partial_ref[keep * capacity + r] = sums([slots + home * capacity + r], values)

    prepare(jnp.zeros((6, LEAF), F32), 3 * slots)
    own.wait()
    beside(group, groups, lambda way, other: along(0, way, other).start())
    arrived(me)
    self_distances(me)

    def in_turn(number):
        step = jnp.where(number > 0, step_of(jnp.maximum(number - 1, 0)), 0)
        return lax.rem(me - step + count, count)

    def relay(number, carry):
        step = step_of(number)
        across(step).wait_recv()
        beside(group, groups, lambda way, other: along(step, way, other).start())
        two_back = in_turn(jnp.maximum(number - 1, 0))
        home = in_turn(number + 1)
        self_sums(two_back, jnp.where(number > 0, two_back, count))
        kernels(capacity, self_dist, self_value)
        arrived(home)
        self_distances(home)
        return carry

    lax.fori_loop(0, count - 1, relay, 0)
    self_sums(in_turn(count - 2), in_turn(count - 2))
    kernels(capacity, self_dist, self_value)
    self_sums(in_turn(count - 1), in_turn(count - 1))

    def side_arrived(step):
        chunk = lax.rem(me - step + count, count)

        def accept(way, other):
            along(step, way, other).wait_recv()
            for r in range(capacity):
                slot = 2 * way * slots + chunk * capacity + r
                prepare(slot_data(2 * way, chunk, r), slot)

        pl.when(group > 0)(lambda: accept(0, group - 1))
        pl.when(group + 1 < groups)(lambda: accept(1, group + 1))

    side_arrived(0)

    def side_relay(number, carry):
        side_arrived(step_of(number))
        return carry

    lax.fori_loop(0, count - 1, side_relay, 0)

    loads[5].wait()
    low = jnp.where(group == 0, slots, 0)
    high = jnp.where(group == groups - 1, 2 * slots, 3 * slots)

    def source(slot, entry):
        named = lists_ref[entry, slot]
        return jnp.where((named >= low) & (named < high), named, 3 * slots)

    def home_of(number):
        step = jnp.where(number < count - 1, step_of(number), 0)
        return lax.rem(me - step + count, count)


    others = range(1, knear)

    def other_distances(home, r):
        slot = home * capacity + r
        for entry in others:
            dist[r][entry - 1] = distances(slot, source(slot, entry))

    def other_sums(home, r, keep):
        slot = home * capacity + r
        total = sums([source(slot, entry) for entry in others], value[r][...])
        total = total + partial_ref[slot]
        x = near_ref[1, home, pl.ds(r, 3, stride=capacity), :]
        flows_ref[keep, pl.ds(r, 3, stride=capacity), :] = total[0:3] + x * total[3:4]

    for r in range(capacity):
        other_distances(home_of(0), r)

    def chunk(number, carry):
        last = jnp.maximum(number - 1, 0)
        before, after = home_of(last), home_of(jnp.minimum(number + 1, count - 1))
        keep = jnp.where(number > 0, before, count)
        for r in range(capacity):
            other_sums(before, r, keep)
            kernels(knear - 1, dist[r], value[r])
            other_distances(after, r)

        @pl.when(number > 0)
        def _():
            across_back(step_of(last)).start()

        return carry

    lax.fori_loop(0, count, chunk, 0)
    for r in range(capacity):
        other_sums(me, r, me)
    back_ref[me] = flows_ref[me]

    def finish(number, carry):
        across_back(step_of(number)).wait_recv()
        return carry

    lax.fori_loop(0, count - 1, finish, 0)

    returned = [
        jnp.concatenate([back_ref[:, k * capacity + r, :] for r in range(capacity)], axis=0)
        for k in range(3)
    ]
    pieces = split3(jnp.concatenate(returned, axis=1))
    taken = sum(jnp.dot(take, piece, preferred_element_type=F32) for piece in pieces)
    tile_rows = [
        jnp.concatenate(
            [
                taken[t * cells : (t + 1) * cells, k * LEAF : (k + 1) * LEAF]
                for k in range(3)
            ],
            axis=0,
        )
        for t in range(tiles)
    ]
    for tile in range(tiles):
        part = tile_rows[tile]
        if tile + 1 < tiles:
            part = jnp.where(lane >= start, part, tile_rows[tile + 1])
        part = turn(part, -1)
        width = min(LEAF, points - tile * LEAF)
        vel_ref[:, tile * LEAF : tile * LEAF + width] = part[:, 0:width]
    stepped = pos_ref[...] + TIME_STEP * vel_ref[...]
    coeffs = product(stepped, ana_high[...], ana_low[...], ((1,), (1,)))
    moved_ref[...] = product(coeffs, syn_high[...], syn_low[...], ((1,), (0,)))

    def sent(number, carry):
        step = step_of(number)
        across(step).wait_send()
        across_back(step).wait_send()
        return carry

    lax.fori_loop(0, count - 1, sent, 0)

    def side_sent(step, carry):
        beside(group, groups, lambda way, other: along(step, way, other).wait_send())
        return carry

    lax.fori_loop(0, count, side_sent, 0)


def shards(positions, analysis, synthesis, stiffness, owner, ulist):
    count = lax.axis_size("dev")
    cells, dims, points = positions.shape
    coefs = analysis.shape[0]
    blocks = owner.shape[0]
    knear = ulist.shape[1]
    capacity = ulist.shape[0] // count
    slots = count * capacity
    rows = dims * cells
    sem = pltpu.SemaphoreType.DMA
    shape = jax.ShapeDtypeStruct((rows, points), F32)
    hbm_spec = pl.BlockSpec(memory_space=pltpu.HBM)
    vmem_spec = pl.BlockSpec(memory_space=pltpu.VMEM)
    moved, velocity = pl.pallas_call(
        functools.partial(kernel, capacity, knear),
        out_shape=(shape, shape),
        in_specs=[hbm_spec] * 6,
        out_specs=(vmem_spec, vmem_spec),
        scratch_shapes=[
            pltpu.SMEM(ulist.T.shape, jnp.int32),
            pltpu.VMEM((rows, points), F32),
            pltpu.VMEM((coefs, points), F32),
            pltpu.VMEM((coefs, points), F32),
            pltpu.VMEM((coefs,), F32),
            pltpu.VMEM((1, blocks), jnp.int32),
            pltpu.VMEM((coefs, points), BF16),
            pltpu.VMEM((coefs, points), BF16),
            pltpu.VMEM((coefs, points), BF16),
            pltpu.VMEM((coefs, points), BF16),
            pltpu.VMEM((count, 6 * capacity, LEAF), F32),
            pltpu.VMEM((3, count, 6 * capacity, LEAF), F32),
            pltpu.VMEM((3 * slots + 1, 64, 2 * LEAF), BF16),
            pltpu.VMEM((slots, LEAF, 48), BF16),
            pltpu.VMEM((count + 1, 3 * capacity, LEAF), F32),
            pltpu.VMEM((count, 3 * capacity, LEAF), F32),
            pltpu.VMEM((capacity, LEAF, 2 * LEAF), F32),
            pltpu.VMEM((LEAF, 4 * capacity * LEAF), BF16),
            pltpu.VMEM((slots + capacity, 8, LEAF), F32),
            *[pltpu.VMEM((knear - 1, LEAF, 2 * LEAF), F32) for _ in range(capacity)],
            *[pltpu.VMEM((LEAF, 4 * (knear - 1) * LEAF), BF16) for _ in range(capacity)],
            sem((6,)), sem, sem((count,)), sem((count,)), sem((2, count)), sem((2, count)),
            sem((count,)), sem((count,)),
        ],
        compiler_params=pltpu.CompilerParams(collective_id=0, has_side_effects=True),
    )(
        ulist.T,
        positions.transpose(1, 0, 2).reshape(rows, points),
        analysis,
        synthesis.T,
        stiffness,
        owner.reshape(1, blocks),
    )

    def to_cells(value):
        return value.reshape(dims, cells, points).transpose(1, 0, 2)

    return to_cells(moved), to_cells(velocity)


def solution(mesh):
    placed = (
        P(("group", "dev"), None, None),
        P(),
        P(),
        P(),
        P(("group", "dev"), None),
        P(("group", "dev"), None),
    )
    return jax.shard_map(
        shards,
        mesh=mesh,
        in_specs=placed,
        out_specs=(P(("group", "dev"), None, None), P(("group", "dev"), None, None)),
        check_vma=False,
    )
```

```python
import functools
import math

import jax
import jax.numpy as jnp
from jax import lax
from jax.experimental import pallas as pl
from jax.experimental.pallas import tpu as pltpu
from jax.sharding import PartitionSpec as P

LEAF = 128
ROWS = 16
SOFTENING = 0.25
ROOT = math.sqrt(SOFTENING)
KERNEL = 1.0 / (8.0 * math.pi)
TIME_STEP = 0.02
MESH = pl.DeviceIdType.MESH
BF16, F32 = jnp.bfloat16, jnp.float32


def split3(value):
    first = value.astype(BF16)
    rest = value - first.astype(F32)
    second = rest.astype(BF16)
    third = (rest - second.astype(F32)).astype(BF16)
    return first, second, third


def split2(value):
    first = value.astype(BF16)
    return first, (value - first.astype(F32)).astype(BF16)


def product(left, right_high, right_low, dims):
    high, low = split2(left)
    dot = functools.partial(
        lax.dot_general, dimension_numbers=(dims, ((), ())), preferred_element_type=F32
    )
    return dot(high, right_high) + (dot(low, right_high) + dot(high, right_low))


def beside(group, groups, action):
    pl.when(group + 1 < groups)(functools.partial(action, 0, group + 1))
    pl.when(group > 0)(functools.partial(action, 1, group - 1))


def kernel(
    capacity, knear,
    lists_hbm, pos_hbm, ana_hbm, syn_hbm, stiff_hbm, owner_hbm,
    moved_ref, vel_ref,
    lists_ref, pos_ref, ana_ref, syn_ref, stiff_ref, owner_ref,
    ana_high, ana_low, syn_high, syn_low,
    packed_ref, near_ref, source_ref, weight_ref, target_ref, flows_ref, back_ref,
    self_dist, self_value, partial_ref, *rest,
):
    dist, value, rest = rest[:capacity], rest[capacity : 2 * capacity], rest[2 * capacity :]
    load_sem, own_sem, send_sem, recv_sem, side_send, side_recv, back_send, back_recv = rest
    count, groups = lax.axis_size("dev"), lax.axis_size("group")
    me, group = lax.axis_index("dev"), lax.axis_index("group")
    slots = count * capacity
    rows, points = pos_ref.shape
    cells = rows // 3
    blocks = owner_ref.shape[1]
    tiles = pl.cdiv(points, LEAF)
    padded = tiles + tiles % 2

    barrier = pltpu.get_barrier_semaphore()

    def signal(step, carry):
        pl.semaphore_signal(
            barrier, inc=1, device_id={"dev": lax.rem(me + step, count)}, device_id_type=MESH
        )
        return carry

    lax.fori_loop(1, count, signal, 0)
    beside(
        group, groups,
        lambda way, other: pl.semaphore_signal(
            barrier, inc=1, device_id={"group": other}, device_id_type=MESH
        ),
    )
    loads = [
        pltpu.make_async_copy(src, dst, load_sem.at[number])
        for number, (src, dst) in enumerate(
            [
                (owner_hbm, owner_ref), (pos_hbm, pos_ref), (ana_hbm, ana_ref),
                (syn_hbm, syn_ref), (stiff_hbm, stiff_ref),
                (lists_hbm, lists_ref),
            ]
        )
    ]
    for load in loads:
        load.start()

    self_value[...] = jnp.zeros_like(self_value)
    for ref in value:
        ref[...] = jnp.zeros_like(ref)

    loads[0].wait()
    piece = lax.broadcasted_iota(jnp.int32, (padded * cells, 1), 0)
    block = (piece % cells) * points // LEAF + piece // cells
    lane_block = lax.broadcasted_iota(jnp.int32, (padded * cells, blocks), 1)
    owner_row = owner_ref[...].astype(F32)
    owner_col = jnp.sum(jnp.where(block == lane_block, owner_row, 0.0), axis=1, keepdims=True)
    earlier = (owner_row == owner_col) & (lane_block < block)
    rank_col = jnp.sum(jnp.where(earlier, 1.0, 0.0), axis=1, keepdims=True)
    place = (rank_col * count + owner_col).astype(jnp.int32)
    place = jnp.where(piece < tiles * cells, place, slots)
    take = place == lax.broadcasted_iota(jnp.int32, (padded * cells, slots), 1)
    take = jnp.where(take, 1.0, 0.0)
    give = take.T.astype(BF16)
    take = take.astype(BF16)

    lane = lax.broadcasted_iota(jnp.int32, (rows, LEAF), 1)
    shift = points % LEAF
    cell = lax.broadcasted_iota(jnp.int32, (rows, LEAF), 0) % cells
    start = cell * shift % LEAF

    def turn(value, way):
        for bit in range((cells - 1).bit_length()):
            amount = way * (shift << bit) % LEAF
            if amount:
                rolled = pltpu.roll(value, amount, 1)
                value = jnp.where(cell // (1 << bit) % 2 == 1, rolled, value)
        return value

    def to_pieces(value):
        pieces, before = [], jnp.zeros((rows, LEAF), F32)
        for tile in range(tiles):
            part = value[:, tile * LEAF : min((tile + 1) * LEAF, points)]
            if part.shape[1] < LEAF:
                blank = jnp.zeros((rows, LEAF - part.shape[1]), F32)
                part = jnp.concatenate([part, blank], axis=1)
            part = turn(part, 1)
            pieces.append(jnp.where(lane >= start, part, before))
            before = part
        pieces += [jnp.zeros((rows, LEAF), F32)] * (padded - tiles)
        return [
            jnp.concatenate([p[k * cells : (k + 1) * cells] for p in pieces], axis=0)
            for k in range(3)
        ]

    def pack(value, first):
        pieces = split3(jnp.concatenate(to_pieces(value), axis=1))
        sent = sum(jnp.dot(give, piece, preferred_element_type=F32) for piece in pieces)
        for k in range(3):
            for r in range(capacity):
                packed_ref[:, (first + k) * capacity + r, :] = sent[
                    r * count : (r + 1) * count, k * LEAF : (k + 1) * LEAF
                ]

    loads[1].wait()
    field = pos_ref[...]
    pack(field, 0)
    loads[2].wait()
    ana_high[...], ana_low[...] = split2(ana_ref[...])
    loads[3].wait()
    syn_high[...], syn_low[...] = split2(syn_ref[...])
    loads[4].wait()
    coeffs = product(field, ana_high[...], ana_low[...], ((1,), (1,)))
    forces = -product(coeffs * stiff_ref[...][None, :], syn_high[...], syn_low[...], ((1,), (0,)))
    pack(forces, 3)

    sides = jnp.minimum(group, 1) + jnp.minimum(groups - 1 - group, 1)
    pl.semaphore_wait(barrier, count - 1 + sides)

    def step_of(number):
        half = (number + 1) // 2
        sign = 2 * (number % 2) - 1
        return count // 2 + sign * half

    def across(step):
        peer = lax.rem(me + step, count)
        return pltpu.make_async_remote_copy(
            src_ref=packed_ref.at[peer],
            dst_ref=near_ref.at[1, me],
            send_sem=send_sem.at[step],
            recv_sem=recv_sem.at[step],
            device_id={"dev": peer},
            device_id_type=MESH,
        )

    def along(step, way, other):
        chunk = lax.rem(me - step + count, count)
        return pltpu.make_async_remote_copy(
            src_ref=near_ref.at[1, chunk],
            dst_ref=near_ref.at[2 * way, chunk],
            send_sem=side_send.at[way, step],
            recv_sem=side_recv.at[way, step],
            device_id={"group": other},
            device_id_type=MESH,
        )

    def across_back(step):
        home = lax.rem(me - step + count, count)
        return pltpu.make_async_remote_copy(
            src_ref=flows_ref.at[home],
            dst_ref=back_ref.at[me],
            send_sem=back_send.at[step],
            recv_sem=back_recv.at[step],
            device_id={"dev": home},
            device_id_type=MESH,
        )

    own = pltpu.make_async_copy(packed_ref.at[me], near_ref.at[1, me], own_sem)
    own.start()

    def send(number, carry):
        across(step_of(number)).start()
        return carry

    lax.fori_loop(0, count - 1, send, 0)

    def prepare(data, slot):
        y, f = data[0:3], data[3:6]
        ones = jnp.ones((1, LEAF), F32)
        zeros3, zeros4 = jnp.zeros((3, LEAF), F32), jnp.zeros((4, LEAF), F32)
        y_sq = jnp.sum(y * y, axis=0, keepdims=True)
        yf = -jnp.sum(y * f, axis=0, keepdims=True)
        scale = 1.0 / SOFTENING
        dist = jnp.concatenate(
            [(-2.0 * scale) * y, scale * y_sq + 1.0, scale * ones, zeros3], axis=0
        )
        proj = jnp.concatenate([f, yf, zeros4], axis=0)
        d1, d2, d3 = [part.astype(F32) for part in split3(dist)]
        p1, p2, p3 = [part.astype(F32) for part in split3(proj)]
        w_f = jnp.concatenate([f * (KERNEL / ROOT), jnp.zeros((5, LEAF), F32)], axis=0)
        cube = KERNEL / ROOT**3
        w_y = jnp.concatenate([-cube * y, cube * ones, zeros4], axis=0)
        f1, f2 = [part.astype(F32) for part in split2(w_f)]
        y1, y2 = [part.astype(F32) for part in split2(w_y)]
        rows_in = [d1, d2, d3, d1, d2, d1, p1, p2, p3, p1, p2, p1]
        source_ref[slot] = jnp.concatenate(rows_in, axis=0).T.astype(BF16)
        weight_ref[slot, :, 0:LEAF] = jnp.concatenate([f1, f2], axis=0).astype(BF16)
        weight_ref[slot, :, LEAF:] = jnp.concatenate([y1, y2], axis=0).astype(BF16)
        return y, y_sq

    def prepare_target(x, x_sq, slot):
        ones = jnp.ones((1, LEAF), F32)
        base = jnp.concatenate([x, ones, x_sq, jnp.zeros((3, LEAF), F32)], axis=0)
        t1, t2, t3 = [part.astype(F32) for part in split3(base)]
        target = jnp.concatenate([t1, t1, t1, t2, t2, t3], axis=0).astype(BF16)
        target_ref[slot, 0:48, 0:LEAF] = target
        target_ref[slot, 48:96, LEAF:] = target
        target_ref[slot, 0:48, LEAF:] = jnp.zeros((48, LEAF), BF16)
        target_ref[slot, 48:96, 0:LEAF] = jnp.zeros((48, LEAF), BF16)

    def slot_data(side, home, r):
        return near_ref[side, home, pl.ds(r, 6, stride=capacity), :]

    def arrived(home):
        for r in range(capacity):
            slot = home * capacity + r
            x, x_sq = prepare(slot_data(1, home, r), slots + slot)
            prepare_target(x, x_sq, slot)

    def distances(slot, numbers):
        sources = [source_ref[number] for number in numbers]
        return jnp.dot(
            jnp.concatenate(sources, axis=0), target_ref[slot], preferred_element_type=F32
        )

    def kernels(items, in_ref, out_ref):
        for item in range(items):
            for row in range(0, LEAF, ROWS):
                at = item * LEAF + row
                rr = in_ref[at : at + ROWS, 0:LEAF]
                projected = in_ref[at : at + ROWS, LEAF:]
                inv = lax.rsqrt(rr)
                inv3 = inv * inv * inv
                parts = split2(inv + inv3) + split2(projected * inv3)
                for part in range(4):
                    at = (4 * item + part) * LEAF + row
                    out_ref[at : at + ROWS] = parts[part]

    def sums(numbers, values):
        weights = []
        for number in numbers:
            w_f = weight_ref[number, :, 0:LEAF]
            w_y = weight_ref[number, :, LEAF:]
            weights += [w_f, w_f, w_y, w_y]
        part = lax.dot_general(
            jnp.concatenate(weights, axis=1),
            values,
            (((1,), (0,)), ((), ())),
            preferred_element_type=F32,
        )
        return part[0:8] + part[8:16]

    def self_distances(home):
        for r in range(capacity):
            slot = home * capacity + r
            self_dist[r * LEAF : (r + 1) * LEAF] = distances(slot, [slots + slot])

    def self_sums(home, keep):
        for r in range(capacity):
            values = self_value[4 * r * LEAF : 4 * (r + 1) * LEAF]
            partial_ref[keep * capacity + r] = sums([slots + home * capacity + r], values)

    prepare(jnp.zeros((6, LEAF), F32), 3 * slots)
    own.wait()
    beside(group, groups, lambda way, other: along(0, way, other).start())
    arrived(me)
    self_distances(me)

    def in_turn(number):
        step = jnp.where(number > 0, step_of(jnp.maximum(number - 1, 0)), 0)
        return lax.rem(me - step + count, count)

    def relay(number, carry):
        step = step_of(number)
        across(step).wait_recv()
        beside(group, groups, lambda way, other: along(step, way, other).start())
        two_back = in_turn(jnp.maximum(number - 1, 0))
        home = in_turn(number + 1)
        self_sums(two_back, jnp.where(number > 0, two_back, count))
        kernels(capacity, self_dist, self_value)
        arrived(home)
        self_distances(home)
        return carry

    lax.fori_loop(0, count - 1, relay, 0)
    self_sums(in_turn(count - 2), in_turn(count - 2))
    kernels(capacity, self_dist, self_value)
    self_sums(in_turn(count - 1), in_turn(count - 1))

    def side_arrived(step):
        chunk = lax.rem(me - step + count, count)

        def accept(way, other):
            along(step, way, other).wait_recv()
            for r in range(capacity):
                slot = 2 * way * slots + chunk * capacity + r
                prepare(slot_data(2 * way, chunk, r), slot)

        pl.when(group > 0)(lambda: accept(0, group - 1))
        pl.when(group + 1 < groups)(lambda: accept(1, group + 1))

    side_arrived(0)

    def side_relay(number, carry):
        side_arrived(step_of(number))
        return carry

    lax.fori_loop(0, count - 1, side_relay, 0)

    loads[5].wait()
    low = jnp.where(group == 0, slots, 0)
    high = jnp.where(group == groups - 1, 2 * slots, 3 * slots)

    def source(slot, entry):
        named = lists_ref[entry, slot]
        return jnp.where((named >= low) & (named < high), named, 3 * slots)

    def home_of(number):
        step = jnp.where(number < count - 1, step_of(number), 0)
        return lax.rem(me - step + count, count)


    others = range(1, knear)

    def other_distances(home, r):
        slot = home * capacity + r
        dist[r][...] = distances(slot, [source(slot, entry) for entry in others])

    def other_sums(home, r, keep):
        slot = home * capacity + r
        total = sums([source(slot, entry) for entry in others], value[r][...])
        total = total + partial_ref[slot]
        x = near_ref[1, home, pl.ds(r, 3, stride=capacity), :]
        flows_ref[keep, pl.ds(r, 3, stride=capacity), :] = total[0:3] + x * total[3:4]

    for r in range(capacity):
        other_distances(home_of(0), r)

    def chunk(number, carry):
        last = jnp.maximum(number - 1, 0)
        before, after = home_of(last), home_of(jnp.minimum(number + 1, count - 1))
        keep = jnp.where(number > 0, before, count)
        for r in range(capacity):
            other_sums(before, r, keep)
            kernels(knear - 1, dist[r], value[r])
            other_distances(after, r)

        @pl.when(number > 0)
        def _():
            across_back(step_of(last)).start()

        return carry

    lax.fori_loop(0, count, chunk, 0)
    for r in range(capacity):
        other_sums(me, r, me)
    back_ref[me] = flows_ref[me]

    def finish(number, carry):
        across_back(step_of(number)).wait_recv()
        return carry

    lax.fori_loop(0, count - 1, finish, 0)

    returned = [
        jnp.concatenate([back_ref[:, k * capacity + r, :] for r in range(capacity)], axis=0)
        for k in range(3)
    ]
    pieces = split3(jnp.concatenate(returned, axis=1))
    taken = sum(jnp.dot(take, piece, preferred_element_type=F32) for piece in pieces)
    tile_rows = [
        jnp.concatenate(
            [
                taken[t * cells : (t + 1) * cells, k * LEAF : (k + 1) * LEAF]
                for k in range(3)
            ],
            axis=0,
        )
        for t in range(tiles)
    ]
    for tile in range(tiles):
        part = tile_rows[tile]
        if tile + 1 < tiles:
            part = jnp.where(lane >= start, part, tile_rows[tile + 1])
        part = turn(part, -1)
        width = min(LEAF, points - tile * LEAF)
        vel_ref[:, tile * LEAF : tile * LEAF + width] = part[:, 0:width]
    stepped = pos_ref[...] + TIME_STEP * vel_ref[...]
    coeffs = product(stepped, ana_high[...], ana_low[...], ((1,), (1,)))
    moved_ref[...] = product(coeffs, syn_high[...], syn_low[...], ((1,), (0,)))

    def sent(number, carry):
        step = step_of(number)
        across(step).wait_send()
        across_back(step).wait_send()
        return carry

    lax.fori_loop(0, count - 1, sent, 0)

    def side_sent(step, carry):
        beside(group, groups, lambda way, other: along(step, way, other).wait_send())
        return carry

    lax.fori_loop(0, count, side_sent, 0)


def shards(positions, analysis, synthesis, stiffness, owner, ulist):
    count = lax.axis_size("dev")
    cells, dims, points = positions.shape
    coefs = analysis.shape[0]
    blocks = owner.shape[0]
    knear = ulist.shape[1]
    capacity = ulist.shape[0] // count
    slots = count * capacity
    rows = dims * cells
    sem = pltpu.SemaphoreType.DMA
    shape = jax.ShapeDtypeStruct((rows, points), F32)
    hbm_spec = pl.BlockSpec(memory_space=pltpu.HBM)
    vmem_spec = pl.BlockSpec(memory_space=pltpu.VMEM)
    moved, velocity = pl.pallas_call(
        functools.partial(kernel, capacity, knear),
        out_shape=(shape, shape),
        in_specs=[hbm_spec] * 6,
        out_specs=(vmem_spec, vmem_spec),
        scratch_shapes=[
            pltpu.SMEM(ulist.T.shape, jnp.int32),
            pltpu.VMEM((rows, points), F32),
            pltpu.VMEM((coefs, points), F32),
            pltpu.VMEM((coefs, points), F32),
            pltpu.VMEM((coefs,), F32),
            pltpu.VMEM((1, blocks), jnp.int32),
            pltpu.VMEM((coefs, points), BF16),
            pltpu.VMEM((coefs, points), BF16),
            pltpu.VMEM((coefs, points), BF16),
            pltpu.VMEM((coefs, points), BF16),
            pltpu.VMEM((count, 6 * capacity, LEAF), F32),
            pltpu.VMEM((3, count, 6 * capacity, LEAF), F32),
            pltpu.VMEM((3 * slots + 1, LEAF, 96), BF16),
            pltpu.VMEM((3 * slots + 1, 16, 2 * LEAF), BF16),
            pltpu.VMEM((slots, 96, 2 * LEAF), BF16),
            pltpu.VMEM((count + 1, 3 * capacity, LEAF), F32),
            pltpu.VMEM((count, 3 * capacity, LEAF), F32),
            pltpu.VMEM((capacity * LEAF, 2 * LEAF), F32),
            pltpu.VMEM((4 * capacity * LEAF, LEAF), BF16),
            pltpu.VMEM((slots + capacity, 8, LEAF), F32),
            *[pltpu.VMEM(((knear - 1) * LEAF, 2 * LEAF), F32) for _ in range(capacity)],
            *[pltpu.VMEM((4 * (knear - 1) * LEAF, LEAF), BF16) for _ in range(capacity)],
            sem((6,)), sem, sem((count,)), sem((count,)), sem((2, count)), sem((2, count)),
            sem((count,)), sem((count,)),
        ],
        compiler_params=pltpu.CompilerParams(collective_id=0, has_side_effects=True),
    )(
        ulist.T,
        positions.transpose(1, 0, 2).reshape(rows, points),
        analysis,
        synthesis.T,
        stiffness,
        owner.reshape(1, blocks),
    )

    def to_cells(value):
        return value.reshape(dims, cells, points).transpose(1, 0, 2)

    return to_cells(moved), to_cells(velocity)


def solution(mesh):
    placed = (
        P(("group", "dev"), None, None),
        P(),
        P(),
        P(),
        P(("group", "dev"), None),
        P(("group", "dev"), None),
    )
    return jax.shard_map(
        shards,
        mesh=mesh,
        in_specs=placed,
        out_specs=(P(("group", "dev"), None, None), P(("group", "dev"), None, None)),
        check_vma=False,
    )
```
